512 devices in a mesh: half: 2 (over core), blk: 64 (over z, y), sub: 4 (over x).
Axes of the slice: x: 4, y: 8, z: 8, core: 2. Of those that a mesh axis runs over, the one named last changes fastest.
Arguments:
- leaf_expansions: float32 [262144, 128], P(('half', 'blk', 'sub')), may hold values from -0.3 to 0.3
- leaf_occupied: int32 [262144], P(('half', 'blk', 'sub')), may hold values 0 or 1
- cone_angles: float32 [2, 768], replicated, may hold values from -3.140625 to 3.140625
- cone_need3: int32 [768, 512], P(('half', 'blk'), 'sub'), may hold values 0 or 1
- cone_need4: int32 [768, 64], P(('half', 'blk'), 'sub'), may hold values 0 or 1
Outputs:
- lowfreq: float32 [4096, 128], P(('half', 'blk', 'sub'))
- cone_expansions: float32 [768, 64, 128], P(('half', 'blk'), 'sub')
The draws below stay inside these ranges and needn't reach their ends.
All inputs are finite; a program needn't handle non-finite values. No bound on the sum of `leaf_occupied` or of `cone_need3` or of `cone_need4` on one device may be relied on, other than what follows from the above.
Results may differ from the reference program's by a relative error of at most 0.00007.
Values sent between devices are 32-bit elements; how exact they have to be, the bound alone decides.
No kernel may reach another device: no remote copies, remote signals or barrier semaphores. Data moves between devices by JAX's collectives and lax.ppermute only.
A program may use at most 64 MiB of HBM per device.

```python
import math
import jax
import jax.numpy as jnp
from jax import lax

ORDER = 4
NODES = 64
CONE_DEV = 6
CONES = 768
LEAF_DEV = 512
LEAVES = 262144
BOX3 = 512
BOX4 = 64
N_HALF = 2
N_BLK = 64
N_SUB = 4


def touch_ends(values, stream_key, smallest, top_value):
    spot = [jax.random.randint(jax.random.fold_in(stream_key, axis), (), 0, length) for axis, length in enumerate(values.shape)]
    longest = values.shape.index(max(values.shape))
    neighbour = spot[:longest] + [(spot[longest] + 1) % values.shape[longest]] + spot[longest + 1:]
    return values.at[tuple(spot)].set(smallest).at[tuple(neighbour)].set(top_value)


def shard_levels(own_key, dims, shards, low, high):
    loudness, own = 1.0, jax.random.fold_in(own_key, 6)
    for dim, parts in shards:
        heights = jnp.exp(jax.random.uniform(jax.random.fold_in(own, dim), (parts,), jnp.float32, low / len(shards), high / len(shards)))
        loudness = loudness * jnp.repeat(heights, dims[dim] // parts).reshape([-1 if axis == dim else 1 for axis in range(len(dims))])
    return loudness


def scatter_about(rng, dims, deviation, most, shards=(), kind=jnp.bfloat16):
    values = deviation * jax.random.normal(rng, dims, jnp.float32)
    if shards:
        values = values * shard_levels(rng, dims, shards, -0.22, 0.18)
    return jnp.clip(values, -most, most).astype(kind)


def setup_inputs(seed: int = 0) -> dict:
    arg_keys = jax.random.split(jax.random.key(seed), 6)
    return {
        "leaf_expansions": scatter_about(arg_keys[0], (LEAVES, 2 * NODES), 0.05, 0.3, ((0, 512),), jnp.float32),
        "leaf_occupied": touch_ends((jax.random.randint(arg_keys[1], (LEAVES,), 0, 2) < 1).astype(jnp.int32), jax.random.fold_in(arg_keys[1], 1), 0, 1),
        "cone_angles": jnp.clip(jax.random.uniform(arg_keys[2], (2, CONES), jnp.float32, -3.140625, 3.140625), -3.140625, 3.140625),
        "cone_need3": touch_ends((jax.random.randint(arg_keys[3], (CONES, BOX3), 0, 4) < 3).astype(jnp.int32), jax.random.fold_in(arg_keys[3], 1), 0, 1),
        "cone_need4": touch_ends((jax.random.randint(arg_keys[4], (CONES, BOX4), 0, 4) < 3).astype(jnp.int32), jax.random.fold_in(arg_keys[4], 1), 0, 1),
    }


near_scale = 1.5
far_scale = 3.0
highest = lax.Precision.HIGHEST


def chebyshev_points(per_axis):
    index = jnp.arange(per_axis, dtype=jnp.float32)
    return jnp.cos((2.0 * index + 1.0) * math.pi / (2.0 * per_axis))


def octant_signs():
    octant = jnp.arange(8, dtype=jnp.int32)
    bits = jnp.stack([(octant // 4) % 2, (octant // 2) % 2, octant % 2], -1)
    return bits.astype(jnp.float32) * 2.0 - 1.0


def octant_table(per_axis):
    points = chebyshev_points(per_axis)
    degree = jnp.arange(1, per_axis, dtype=jnp.float32)
    sign_pair = jnp.array([-1.0, 1.0], dtype=jnp.float32)
    shifted = (points[None, :] + sign_pair[:, None]) / 2.0
    poly_here = jnp.cos(degree[None, :] * jnp.arccos(points)[:, None])
    poly_there = jnp.cos(degree[None, None, :] * jnp.arccos(shifted)[:, :, None])
    single = 1.0 / per_axis + (2.0 / per_axis) * jnp.einsum('mk,bnk->bmn', poly_here, poly_there, precision=highest)
    signs = octant_signs()
    along_x = jnp.where((signs[:, 0] > 0)[:, None, None], single[1][None], single[0][None])
    along_y = jnp.where((signs[:, 1] > 0)[:, None, None], single[1][None], single[0][None])
    along_z = jnp.where((signs[:, 2] > 0)[:, None, None], single[1][None], single[0][None])
    full = jnp.einsum('oad,obe,ocf->odefabc', along_x, along_y, along_z, precision=highest)
    node_count = per_axis ** 3
    return full.reshape(8, node_count, node_count)


def node_offsets(per_axis):
    points = chebyshev_points(per_axis)
    index = jnp.arange(per_axis ** 3, dtype=jnp.int32)
    coords = jnp.stack([points[index // (per_axis * per_axis)], points[(index // per_axis) % per_axis], points[index % per_axis]], -1)
    return coords[None, :, :] + octant_signs()[:, None, :]


def phases(angles, strength, per_axis):
    polar = angles[0]
    azimuth = angles[1]
    direction = jnp.stack([jnp.sin(polar) * jnp.cos(azimuth), jnp.sin(polar) * jnp.sin(azimuth), jnp.cos(polar)], -1)
    offsets = node_offsets(per_axis)
    argument = offsets[None, :, :, 0] * direction[:, None, None, 0]
    argument = argument + offsets[None, :, :, 1] * direction[:, None, None, 1]
    argument = argument + offsets[None, :, :, 2] * direction[:, None, None, 2]
    argument = -strength * argument
    return jnp.cos(argument), jnp.sin(argument)


def interpolate(real_part, imag_part, cosines, sine_part, transfer):
    mod_real = cosines * real_part - sine_part * imag_part
    mod_imag = cosines * imag_part + sine_part * real_part
    out_real = jnp.einsum('...on,onm->...m', mod_real, transfer, precision=highest)
    out_imag = jnp.einsum('...on,onm->...m', mod_imag, transfer, precision=highest)
    return out_real, out_imag


def reference(leaf_expansions, leaf_occupied, cone_angles, cone_need3, cone_need4):
    node_count = NODES
    groups = N_HALF * N_BLK
    level_one_count = LEAF_DEV // 8
    pair_count = level_one_count // 2
    per_sub = pair_count // N_SUB
    per_box = per_sub // 8
    transfer = octant_table(ORDER)
    masked = leaf_expansions * leaf_occupied.astype(jnp.float32)[:, None]
    masked = masked.reshape(groups, N_SUB, level_one_count, 8, 2, node_count)
    level_one = jnp.einsum('gspoan,onm->gspam', masked, transfer, precision=highest)
    level_one = level_one.reshape(groups, N_SUB, pair_count, 2, 2, node_count)
    level_one = jnp.transpose(level_one, (0, 2, 1, 3, 4, 5)).reshape(groups, pair_count, 2 * N_SUB, 2, node_count)
    level_two = jnp.einsum('gkoan,onm->gkam', level_one, transfer[:2 * N_SUB], precision=highest)
    lowfreq = level_two.reshape(groups * pair_count, 2 * node_count)
    box_rows = level_two.reshape(groups, N_SUB, per_box, 8, 2, node_count)
    box_rows = jnp.transpose(box_rows, (1, 0, 2, 3, 4, 5)).reshape(N_SUB * groups * per_box, 8, 2, node_count)
    real_part = box_rows[:, :, 0, :]
    imag_part = box_rows[:, :, 1, :]
    angle_blocks = jnp.transpose(cone_angles.reshape(2, groups, CONE_DEV), (1, 0, 2))
    need_three = cone_need3.reshape(groups, CONE_DEV, -1)
    need_four = cone_need4.reshape(groups, CONE_DEV, -1)

    def one_block(inputs):
        angles, mask_three, mask_four = inputs
        cos_near, sin_near = phases(angles, near_scale, ORDER)
        three_real, three_imag = interpolate(real_part[None], imag_part[None], cos_near[:, None], sin_near[:, None], transfer)
        weight = mask_three.astype(jnp.float32)[:, :, None]
        three_real = three_real * weight
        three_imag = three_imag * weight
        shape_six = (CONE_DEV, N_SUB, groups // 8, 8, per_box, node_count)
        three_real = jnp.transpose(three_real.reshape(shape_six), (0, 1, 2, 4, 3, 5)).reshape(CONE_DEV, -1, 8, node_count)
        three_imag = jnp.transpose(three_imag.reshape(shape_six), (0, 1, 2, 4, 3, 5)).reshape(CONE_DEV, -1, 8, node_count)
        cos_far, sin_far = phases(angles, far_scale, ORDER)
        four_real, four_imag = interpolate(three_real, three_imag, cos_far[:, None], sin_far[:, None], transfer)
        joined = jnp.concatenate([four_real, four_imag], -1)
        return joined * mask_four.astype(jnp.float32)[:, :, None]

    cone_expansions = lax.map(one_block, (angle_blocks, need_three, need_four))
    cone_expansions = cone_expansions.reshape(CONES, -1, 2 * node_count)
    return lowfreq, cone_expansions
```

```python
import math

import jax
import jax.numpy as jnp
import numpy as np
from jax import lax
from jax.experimental import pallas as pl
from jax.experimental.pallas import tpu as pltpu
from jax.sharding import Mesh
from jax.sharding import PartitionSpec as P

ORDER = 4
NODES = ORDER**3
OCTANTS = 8
WIDTH = 2 * NODES
NEAR = 1.5
f32 = jnp.float32
bf16 = jnp.bfloat16


def points():
    index = np.arange(ORDER, dtype=np.float64)
    return np.cos((2.0 * index + 1.0) * math.pi / (2.0 * ORDER))


def transfer_parts():
    here = points()
    degree = np.arange(1, ORDER)
    single = []
    for sign in (-1.0, 1.0):
        there = (here + sign) / 2.0
        poly_here = np.cos(degree[None, :] * np.arccos(here)[:, None])
        poly_there = np.cos(degree[None, :] * np.arccos(there)[:, None])
        single.append(1.0 / ORDER + 2.0 / ORDER * poly_there @ poly_here.T)
    rows = []
    for octant in range(OCTANTS):
        along = [single[octant // 4 % 2], single[octant // 2 % 2], single[octant % 2]]
        full = np.kron(np.kron(along[0], along[1]), along[2])
        rows.append(np.kron(np.eye(2), full))
    table = np.concatenate(rows).astype(np.float32)
    high = table.astype(bf16)
    low = (table - high.astype(np.float32)).astype(bf16)
    return np.concatenate([high, low], 1)


def lane_points():
    here = points()
    index = np.arange(NODES)
    coords = np.stack([here[index // ORDER**2], here[index // ORDER % ORDER], here[index % ORDER]])
    coords = NEAR * np.concatenate([coords, -coords], 1)
    sign = np.concatenate([np.ones(NODES), -np.ones(NODES)])[None]
    pad = np.zeros((4, WIDTH))
    return np.concatenate([coords, sign, pad]).astype(np.float32)


def split(value):
    high = value.astype(bf16)
    low = (value - high.astype(f32)).astype(bf16)
    return high, low


def joined(product, rows):
    top = product[:rows]
    bottom = product[rows:]
    return top[:, :WIDTH] + (top[:, WIDTH:] + bottom[:, :WIDTH]) + bottom[:, WIDTH:]


def times(value, weights):
    high, low = split(value)
    product = jnp.dot(jnp.concatenate([high, low]), weights, preferred_element_type=f32)
    return joined(product, value.shape[0])


def leaf_kernel(place, occupied, leaves, weights, out, masked, first):
    rows = leaves.shape[0]
    for block in range(rows // 128):
        line = occupied[block : block + 1, :].astype(f32)
        column = jnp.transpose(jnp.broadcast_to(line, (128, 128)))
        masked[pl.ds(128 * block, 128), :] = leaves[pl.ds(128 * block, 128), :] * column
    boxes = rows // OCTANTS
    parts = [masked[pl.ds(o, boxes, stride=OCTANTS), :] for o in range(OCTANTS)]
    first[...] = times(jnp.concatenate(parts, 1), weights[...])
    pairs = [first[pl.ds(r, boxes // 2, stride=2), :] for r in range(2)]
    start = pl.multiple_of(place[0] * (2 * WIDTH), 2 * WIDTH)
    own = weights[pl.ds(start, 2 * WIDTH), :]
    second = times(jnp.concatenate(pairs, 1), own)
    chunks = second.reshape(out.shape[1:])
    for copy in range(out.shape[0]):
        out[copy] = chunks


def phase_kernel(place, angles, lanes, cosines, sines):
    cones = cosines.shape[0]
    total = angles.shape[1]
    mine = OCTANTS * (cones // 16) // OCTANTS
    row = lax.broadcasted_iota(jnp.int32, (cones, total), 0)
    col = lax.broadcasted_iota(jnp.int32, (cones, total), 1)
    group = row // mine
    wanted = (group * OCTANTS + place[0]) * mine + (row - group * mine)
    pick = (col == wanted).astype(f32)
    chosen = lax.dot_general(
        pick,
        angles[...],
        (((1,), (1,)), ((), ())),
        precision=lax.Precision.HIGHEST,
        preferred_element_type=f32,
    )
    sin_a = jnp.sin(chosen)
    cos_a = jnp.cos(chosen)
    direct = [
        sin_a[:, 0:1] * cos_a[:, 1:2],
        sin_a[:, 0:1] * sin_a[:, 1:2],
        cos_a[:, 0:1],
    ]
    argument = direct[0] * lanes[0:1, :] + direct[1] * lanes[1:2, :] + direct[2] * lanes[2:3, :]
    base = (jnp.cos(argument), jnp.sin(argument))
    steps = []
    for d in range(3):
        angle = jnp.broadcast_to(direct[d] * NEAR, (cones, WIDTH)) * lanes[3:4, :]
        steps.append((jnp.cos(angle), jnp.sin(angle)))

    def turned(value, step, sign):
        c, s = value
        a, b = step
        if sign > 0:
            return (c * a - s * b, s * a + c * b)
        return (c * a + s * b, s * a - c * b)

    for octant in range(OCTANTS):
        bits = (octant // 4 % 2, octant // 2 % 2, octant % 2)
        value = base
        for d in range(3):
            value = turned(value, steps[d], 2 * bits[d] - 1)
        cosines[:, octant * WIDTH : (octant + 1) * WIDTH] = value[0]
        sines[:, octant * WIDTH : (octant + 1) * WIDTH] = value[1]


def level_kernel(place, received, cosines, sines, need, weights, out, lowfreq, operand, mask):
    cones = cosines.shape[0]
    groups = need.shape[0]
    mine = cones // groups
    subs = received.shape[0] // OCTANTS
    low_own = received[subs * place[0]]
    for s in range(1, subs):
        low_own = low_own + received[subs * place[0] + s]
    lowfreq[...] = low_own
    for g in range(groups):
        mask[pl.ds(g * mine, mine), :] = need[g, :mine, :]
    for y in range(OCTANTS):
        box = received[subs * y]
        for s in range(1, subs):
            box = box + received[subs * y + s]
        turned = pltpu.roll(box, NODES, 1)
        for o in range(OCTANTS):
            at = pl.ds(o * WIDTH, WIDTH)
            value = cosines[:, at] * box[o : o + 1, :] + sines[:, at] * turned[o : o + 1, :]
            high, low = split(value)
            operand[pl.ds(2 * cones * y, cones), at] = high
            operand[pl.ds(2 * cones * y + cones, cones), at] = low
    product = jnp.dot(operand[...], weights[...], preferred_element_type=f32)
    shift = lax.rem(2 * WIDTH - place[1] * OCTANTS, WIDTH)
    needed = pltpu.roll(mask[...], shift, 1)
    parts = []
    for y in range(OCTANTS):
        at = pl.ds(y * WIDTH, WIDTH)
        three = joined(product[2 * cones * y : 2 * cones * (y + 1)], cones)
        three = three * needed[:, y : y + 1]
        c = cosines[:, at]
        s = sines[:, at]
        parts.append((c * c - s * s) * three + (2.0 * c * s) * pltpu.roll(three, NODES, 1))
    four = times(jnp.concatenate(parts, 1), weights[...])
    for g in range(groups):
        out[g, :mine, :] = four[g * mine : (g + 1) * mine]


def vmem():
    return pl.BlockSpec(memory_space=pltpu.VMEM)


def smem():
    return pl.BlockSpec(memory_space=pltpu.SMEM)


def local(leaf_expansions, leaf_occupied, cone_angles, cone_need3, cone_need4):
    rows, width = leaf_expansions.shape
    cone_local = cone_need3.shape[0]
    subs = lax.axis_size("sub")
    eights = lax.axis_size("y")
    groups = lax.axis_size("half") * lax.axis_size("z")
    cones = groups * cone_local
    weights = jnp.asarray(transfer_parts())
    lanes = jnp.asarray(lane_points())
    y_place = lax.axis_index("y")
    group_place = lax.axis_index(("half", "z"))
    partial = pl.pallas_call(
        leaf_kernel,
        out_shape=jax.ShapeDtypeStruct((eights, subs, 8, width), f32),
        in_specs=[smem(), vmem(), vmem(), vmem()],
        out_specs=vmem(),
        scratch_shapes=[pltpu.VMEM((rows, width), f32), pltpu.VMEM((rows // 8, width), f32)],
        name="leaves",
    )(
        lax.axis_index("sub").reshape(1),
        leaf_occupied.reshape(rows // 128, 128),
        leaf_expansions,
        weights,
    )
    received = lax.all_to_all(
        partial.reshape(eights * subs, 8, width),
        ("y", "sub"),
        split_axis=0,
        concat_axis=0,
        tiled=True,
    )
    need = jnp.pad(cone_need3.astype(f32), ((0, 8 - cone_local), (0, 0)))
    need = lax.all_to_all(
        jnp.broadcast_to(need[None], (groups, 8, need.shape[1])),
        ("half", "z"),
        split_axis=0,
        concat_axis=0,
        tiled=True,
    )
    cosines, sines = pl.pallas_call(
        phase_kernel,
        out_shape=[jax.ShapeDtypeStruct((cones, OCTANTS * width), f32)] * 2,
        in_specs=[smem(), vmem(), vmem()],
        out_specs=[vmem(), vmem()],
        name="phases",
    )(y_place.reshape(1), cone_angles, lanes)
    four, lowfreq = pl.pallas_call(
        level_kernel,
        out_shape=[
            jax.ShapeDtypeStruct((groups, 8, width), f32),
            jax.ShapeDtypeStruct((8, width), f32),
        ],
        in_specs=[smem()] + [vmem()] * 5,
        out_specs=[vmem(), vmem()],
        scratch_shapes=[
            pltpu.VMEM((2 * cones * OCTANTS, OCTANTS * width), bf16),
            pltpu.VMEM((cones, width), f32),
        ],
        name="levels",
    )(jnp.stack([y_place, group_place]), received, cosines, sines, need, weights)
    four = lax.all_to_all(four, ("half", "z"), split_axis=0, concat_axis=0, tiled=True)
    four = jnp.transpose(four[:, :cone_local, :], (1, 0, 2))
    return (lowfreq, four * cone_need4.astype(f32)[:, :, None])


def solution(mesh):
    halves, blocks, subs = mesh.devices.shape
    fine = Mesh(
        mesh.devices.reshape(halves, blocks // OCTANTS, OCTANTS, subs), ("half", "z", "y", "sub")
    )
    blk = ("half", "z", "y")
    return jax.shard_map(
        local,
        mesh=fine,
        in_specs=(
            P(blk + ("sub",), None),
            P(blk + ("sub",)),
            P(),
            P(blk, "sub"),
            P(blk, "sub"),
        ),
        out_specs=(P(blk + ("sub",), None), P(blk, "sub", None)),
        check_vma=False,
    )
```

```python
import math

import jax
import jax.numpy as jnp
import numpy as np
from jax import lax
from jax.experimental import pallas as pl
from jax.experimental.pallas import tpu as pltpu
from jax.sharding import Mesh
from jax.sharding import PartitionSpec as P

ORDER = 4
NODES = ORDER**3
OCTANTS = 8
WIDTH = 2 * NODES
NEAR = 1.5
FAR = 3.0
f32 = jnp.float32
bf16 = jnp.bfloat16


def points():
    index = np.arange(ORDER, dtype=np.float64)
    return np.cos((2.0 * index + 1.0) * math.pi / (2.0 * ORDER))


def transfer_rows():
    here = points()
    degree = np.arange(1, ORDER)
    single = []
    for sign in (-1.0, 1.0):
        there = (here + sign) / 2.0
        poly_here = np.cos(degree[None, :] * np.arccos(here)[:, None])
        poly_there = np.cos(degree[None, :] * np.arccos(there)[:, None])
        single.append(1.0 / ORDER + 2.0 / ORDER * poly_there @ poly_here.T)
    rows, quarters = [], []
    for octant in range(OCTANTS):
        along = [single[octant // 4 % 2], single[octant // 2 % 2], single[octant % 2]]
        full = np.kron(np.kron(along[0], along[1]), along[2])
        rows.append(np.kron(np.eye(2), full))
        quarters.append(np.kron(np.ones((2, 2)), full))
    table = np.concatenate(rows).astype(np.float32)
    high = table.astype(bf16)
    low = (table - high.astype(np.float32)).astype(bf16)
    return np.concatenate([high, low], 1), np.concatenate(quarters).astype(np.float32)


def near_columns():
    here = points()
    index = np.arange(NODES)
    coords = np.stack([here[index // ORDER**2], here[index // ORDER % ORDER], here[index % ORDER]])
    return np.tile(NEAR * coords.reshape(-1, 1), (1, WIDTH)).astype(np.float32)


def octant_rows():
    here = points()
    index = np.arange(NODES)
    coords = np.stack([here[index // ORDER**2], here[index // ORDER % ORDER], here[index % ORDER]])
    coords = np.concatenate([coords, coords], 1)
    octant = np.arange(OCTANTS)
    signs = np.stack([octant // 4 % 2, octant // 2 % 2, octant % 2]) * 2.0 - 1.0
    near = np.tile(NEAR * signs[:, :, None], (1, 1, WIDTH))
    far = FAR * (coords[:, None, :] + signs[:, :, None])
    return np.concatenate([near, far]).astype(np.float32).reshape(-1, WIDTH)


def split(value):
    high = value.astype(bf16)
    low = (value - high.astype(f32)).astype(bf16)
    return high, low


def joined(product, rows):
    top = product[:rows]
    bottom = product[rows:]
    return top[:, :WIDTH] + (top[:, WIDTH:] + bottom[:, :WIDTH]) + bottom[:, WIDTH:]


def times(value, weights):
    high, low = split(value)
    product = jnp.dot(jnp.concatenate([high, low]), weights, preferred_element_type=f32)
    return joined(product, value.shape[0])


def leaf_kernel(place, occupied, leaves, weights, out, masked, first):
    rows = leaves.shape[0]
    for block in range(rows // 128):
        line = occupied[block : block + 1, :].astype(f32)
        column = jnp.transpose(jnp.broadcast_to(line, (128, 128)))
        masked[pl.ds(128 * block, 128), :] = leaves[pl.ds(128 * block, 128), :] * column
    boxes = rows // OCTANTS
    parts = [masked[pl.ds(o, boxes, stride=OCTANTS), :] for o in range(OCTANTS)]
    first[...] = times(jnp.concatenate(parts, 1), weights[...])
    pairs = [first[pl.ds(r, boxes // 2, stride=2), :] for r in range(2)]
    start = pl.multiple_of(place[0] * (2 * WIDTH), 2 * WIDTH)
    own = weights[pl.ds(start, 2 * WIDTH), :]
    second = times(jnp.concatenate(pairs, 1), own)
    out[...] = second.reshape(out.shape)


def cosine_sine(x):
    turns = jnp.floor(x * (2.0 / math.pi) + 0.5)
    r = x - turns * 1.5703125
    r = r - turns * 4.837512969970703125e-4
    r = r - turns * 7.54978995489188216e-8
    z = r * r
    sine = r + r * z * (-1.6666654611e-1 + z * (8.3321608736e-3 - z * 1.9515295891e-4))
    cosine = 4.166664568298827e-2 + z * (-1.388731625493765e-3 + z * 2.443315711809948e-5)
    cosine = 1.0 - 0.5 * z + z * z * cosine
    quarter = turns.astype(jnp.int32)
    swap = (quarter & 1) == 1
    c = jnp.where(swap, sine, cosine)
    s = jnp.where(swap, cosine, sine)
    return jnp.where(((quarter + 1) & 2) == 2, -c, c), jnp.where((quarter & 2) == 2, -s, s)


def column_of(rows):
    count, width = rows.shape
    flags = jnp.concatenate([rows, jnp.zeros((WIDTH - count, width), f32)])
    if width < WIDTH:
        flags = jnp.concatenate([flags, jnp.zeros((WIDTH, WIDTH - width), f32)], 1)
    turned = jnp.transpose(flags)
    return [jnp.broadcast_to(turned[:width, c : c + 1], (width, WIDTH)) for c in range(count)]


def table_kernel(
    place, angles, need_three, need_four, columns, octants, quarters, high, low, far_cos, far_sin, keep
):
    cones = need_three.shape[0]
    row = lax.broadcasted_iota(jnp.int32, (8, WIDTH), 0)
    polar = jnp.zeros((8, WIDTH), f32)
    azimuth = jnp.zeros((8, WIDTH), f32)
    for c in range(cones):
        polar = jnp.where(row == c, angles[0, place[0] * cones + c], polar)
        azimuth = jnp.where(row == c, angles[1, place[0] * cones + c], azimuth)
    cos_p, sin_p = cosine_sine(polar)
    cos_a, sin_a = cosine_sine(azimuth)
    direction = (sin_p * cos_a, sin_p * sin_a, cos_p)
    real = lax.broadcasted_iota(jnp.int32, (NODES, WIDTH), 1) < NODES
    three_flags = column_of(need_three[...].astype(f32))
    four_flags = column_of(need_four[...].astype(f32))
    boxes = need_four.shape[1]
    for c in range(cones):
        along = [direction[d][c : c + 1, :] for d in range(3)]

        def dot(table, start, size):
            value = along[0] * table[start : start + size, :]
            value = value + along[1] * table[start + size : start + 2 * size, :]
            return value + along[2] * table[start + 2 * size : start + 3 * size, :]

        c0, s0 = cosine_sine(dot(columns, 0, NODES))
        ways = (
            (jnp.where(real, c0, -s0), jnp.where(real, -s0, -c0)),
            (jnp.where(real, s0, c0), jnp.where(real, c0, -s0)),
        )
        c1, s1 = cosine_sine(dot(octants, 0, OCTANTS))
        for o in range(OCTANTS):
            for part in range(2):
                at = pl.ds(o * WIDTH + part * NODES, NODES)
                value = ways[part][0] * c1[o : o + 1, :] + ways[part][1] * s1[o : o + 1, :]
                top, rest = split(value * quarters[at, :])
                high[at, c * WIDTH : (c + 1) * WIDTH] = top
                low[at, c * WIDTH : (c + 1) * WIDTH] = rest
        c3, s3 = cosine_sine(dot(octants, 3 * OCTANTS, OCTANTS))
        s3 = jnp.where(real[:OCTANTS], s3, -s3)
        at = pl.ds(c * WIDTH, WIDTH)
        far_cos[at, :] = jnp.concatenate([c3] * boxes) * three_flags[c]
        far_sin[at, :] = jnp.concatenate([s3] * boxes) * three_flags[c]
        keep[pl.ds(c * boxes, boxes), :] = four_flags[c]


def level_kernel(gathered, high, low, far_cos, far_sin, keep, weights, out, turned):
    boxes = gathered.shape[0] // OCTANTS
    rows = keep.shape[0]
    parts = [gathered[pl.ds(o, boxes, stride=OCTANTS), :] for o in range(OCTANTS)]
    top, rest = split(jnp.concatenate(parts, 1))
    both = jnp.dot(jnp.concatenate([top, rest]), high[...], preferred_element_type=f32)
    three = both[:boxes] + (both[boxes:] + jnp.dot(top, low[...], preferred_element_type=f32))
    for c in range(three.shape[1] // WIDTH):
        at = pl.ds(c * boxes, boxes)
        value = three[:, c * WIDTH : (c + 1) * WIDTH]
        turned[at, :] = far_cos[at, :] * value + far_sin[at, :] * pltpu.roll(value, NODES, 1)
    parts = [turned[pl.ds(o, rows, stride=OCTANTS), :] for o in range(OCTANTS)]
    four = times(jnp.concatenate(parts, 1), weights[...])
    out[...] = (four * keep[...]).reshape(out.shape)


def vmem():
    return pl.BlockSpec(memory_space=pltpu.VMEM)


def smem():
    return pl.BlockSpec(memory_space=pltpu.SMEM)


def here(array):
    return pltpu.with_memory_space_constraint(array, pltpu.VMEM)


def local(leaf_expansions, leaf_occupied, cone_angles, cone_need3, cone_need4):
    rows, width = leaf_expansions.shape
    cones, boxes = cone_need3.shape
    fours = cone_need4.shape[1]
    subs = lax.axis_size("sub")
    blocks = lax.axis_size("z") * lax.axis_size("y")
    parts, quarters = transfer_rows()
    weights = jnp.asarray(parts)
    partial = pl.pallas_call(
        leaf_kernel,
        out_shape=jax.ShapeDtypeStruct((subs, 8, width), f32),
        in_specs=[smem(), vmem(), vmem(), vmem()],
        out_specs=vmem(),
        scratch_shapes=[pltpu.VMEM((rows, width), f32), pltpu.VMEM((rows // 8, width), f32)],
        compiler_params=pltpu.CompilerParams(vmem_limit_bytes=24 << 20),
        name="leaves",
    )(
        lax.axis_index("sub").reshape(1),
        leaf_occupied.reshape(rows // 128, 128),
        leaf_expansions,
        weights,
    )
    received = lax.all_to_all(partial, "sub", split_axis=0, concat_axis=0, tiled=True)
    tables = pl.pallas_call(
        table_kernel,
        out_shape=[
            pltpu.VMEM((OCTANTS * width, cones * width), bf16),
            pltpu.VMEM((OCTANTS * width, cones * width), bf16),
            pltpu.VMEM((cones * boxes, width), f32),
            pltpu.VMEM((cones * boxes, width), f32),
            pltpu.VMEM((cones * fours, width), f32),
        ],
        in_specs=[smem(), smem()] + [vmem()] * 5,
        out_specs=[vmem()] * 5,
        compiler_params=pltpu.CompilerParams(vmem_limit_bytes=24 << 20),
        name="tables",
    )(
        lax.axis_index(("half", "z", "y")).reshape(1),
        cone_angles,
        cone_need3,
        cone_need4,
        jnp.asarray(near_columns()),
        jnp.asarray(octant_rows()),
        jnp.asarray(quarters),
    )
    received, *tables = lax.optimization_barrier((received, *tables))
    lowfreq = received.sum(axis=0)
    gathered = lax.all_to_all(
        jnp.broadcast_to(lowfreq[None], (blocks, 8, width)),
        ("z", "y"),
        split_axis=0,
        concat_axis=0,
        tiled=True,
    )
    gathered = lax.all_gather(gathered.reshape(blocks * 8, width), "half", tiled=True)
    cone_expansions = pl.pallas_call(
        level_kernel,
        out_shape=jax.ShapeDtypeStruct((cones, fours, width), f32),
        in_specs=[vmem()] * 7,
        out_specs=vmem(),
        scratch_shapes=[pltpu.VMEM((cones * boxes, width), f32)],
        compiler_params=pltpu.CompilerParams(vmem_limit_bytes=24 << 20),
        name="levels",
    )(here(gathered), *[here(table) for table in tables], weights)
    return (lowfreq, cone_expansions)


def solution(mesh):
    halves, blocks, subs = mesh.devices.shape
    fine = Mesh(
        mesh.devices.reshape(halves, blocks // OCTANTS, OCTANTS, subs), ("half", "z", "y", "sub")
    )
    blk = ("half", "z", "y")
    return jax.shard_map(
        local,
        mesh=fine,
        in_specs=(
            P(blk + ("sub",), None),
            P(blk + ("sub",)),
            P(),
            P(blk, "sub"),
            P(blk, "sub"),
        ),
        out_specs=(P(blk + ("sub",), None), P(blk, "sub", None)),
        check_vma=False,
    )
```

```python
import math

import jax
import jax.numpy as jnp
import numpy as np
from jax import lax
from jax.experimental import pallas as pl
from jax.experimental.pallas import tpu as pltpu
from jax.sharding import Mesh
from jax.sharding import PartitionSpec as P

ORDER = 4
NODES = ORDER**3
OCTANTS = 8
WIDTH = 2 * NODES
NEAR = 1.5
FAR = 3.0
f32 = jnp.float32
bf16 = jnp.bfloat16


def points():
    index = np.arange(ORDER, dtype=np.float64)
    return np.cos((2.0 * index + 1.0) * math.pi / (2.0 * ORDER))


def transfer_rows():
    here = points()
    degree = np.arange(1, ORDER)
    single = []
    for sign in (-1.0, 1.0):
        there = (here + sign) / 2.0
        poly_here = np.cos(degree[None, :] * np.arccos(here)[:, None])
        poly_there = np.cos(degree[None, :] * np.arccos(there)[:, None])
        single.append(1.0 / ORDER + 2.0 / ORDER * poly_there @ poly_here.T)
    rows, quarters = [], []
    for octant in range(OCTANTS):
        along = [single[octant // 4 % 2], single[octant // 2 % 2], single[octant % 2]]
        full = np.kron(np.kron(along[0], along[1]), along[2])
        rows.append(np.kron(np.eye(2), full))
        quarters.append(np.kron(np.ones((1, 2)), full))
    table = np.concatenate(rows).astype(np.float32)
    high = table.astype(bf16)
    low = (table - high.astype(np.float32)).astype(bf16)
    return np.concatenate([high, low], 1), np.concatenate(quarters).astype(np.float32)


def near_columns():
    here = points()
    index = np.arange(NODES)
    coords = np.stack([here[index // ORDER**2], here[index // ORDER % ORDER], here[index % ORDER]])
    return np.tile(NEAR * coords.reshape(-1, 1), (1, WIDTH)).astype(np.float32)


def octant_rows():
    here = points()
    index = np.arange(NODES)
    coords = np.stack([here[index // ORDER**2], here[index // ORDER % ORDER], here[index % ORDER]])
    coords = np.concatenate([coords, coords], 1)
    octant = np.arange(OCTANTS)
    signs = np.stack([octant // 4 % 2, octant // 2 % 2, octant % 2]) * 2.0 - 1.0
    near = np.tile(NEAR * signs[:, :, None], (1, 1, WIDTH))
    far = FAR * (coords[:, None, :] + signs[:, :, None])
    return np.concatenate([near, far]).astype(np.float32).reshape(-1, WIDTH)


def split(value):
    high = value.astype(bf16)
    low = (value - high.astype(f32)).astype(bf16)
    return high, low


def joined(product, rows):
    top = product[:rows]
    bottom = product[rows:]
    return top[:, :WIDTH] + (top[:, WIDTH:] + bottom[:, :WIDTH]) + bottom[:, WIDTH:]


def times(value, weights):
    high, low = split(value)
    product = jnp.dot(jnp.concatenate([high, low]), weights, preferred_element_type=f32)
    return joined(product, value.shape[0])


def leaf_kernel(
    place,
    occupied_far,
    narrow_far,
    leaves_far,
    out,
    occupied,
    narrow,
    leaves,
    weights,
    masked,
    first,
    sems,
):
    copies = [
        pltpu.make_async_copy(far, near, sems.at[i])
        for i, (far, near) in enumerate(
            ((occupied_far, occupied), (narrow_far, narrow), (leaves_far, leaves))
        )
    ]
    for copy in copies:
        copy.start()
    rows = leaves.shape[0]
    copies[0].wait()
    columns = []
    for block in range(rows // WIDTH):
        line = occupied[block : block + 1, :].astype(f32)
        columns.append(jnp.transpose(jnp.broadcast_to(line, (WIDTH, WIDTH))))
    copies[1].wait()
    real = lax.broadcasted_iota(jnp.int32, (NODES, WIDTH), 1) < NODES
    for o in range(OCTANTS):
        value = narrow[o * NODES : (o + 1) * NODES, :].astype(f32)
        other = pltpu.roll(value, NODES, 1)
        top = pl.ds(o * WIDTH, NODES)
        bottom = pl.ds(o * WIDTH + NODES, NODES)
        weights[top, :WIDTH] = jnp.where(real, value, 0.0).astype(bf16)
        weights[top, WIDTH:] = jnp.where(real, other, 0.0).astype(bf16)
        weights[bottom, :WIDTH] = jnp.where(real, 0.0, other).astype(bf16)
        weights[bottom, WIDTH:] = jnp.where(real, 0.0, value).astype(bf16)
    copies[2].wait()
    for block in range(rows // WIDTH):
        at = pl.ds(WIDTH * block, WIDTH)
        masked[at, :] = leaves[at, :] * columns[block]
    boxes = rows // OCTANTS
    parts = [masked[pl.ds(o, boxes, stride=OCTANTS), :] for o in range(OCTANTS)]
    first[...] = times(jnp.concatenate(parts, 1), weights[...])
    pairs = [first[pl.ds(r, boxes // 2, stride=2), :] for r in range(2)]
    start = pl.multiple_of(place[0] * (2 * WIDTH), 2 * WIDTH)
    own = weights[pl.ds(start, 2 * WIDTH), :]
    second = times(jnp.concatenate(pairs, 1), own)
    out[...] = second.reshape(out.shape)


def cosine_sine(x):
    turns = jnp.floor(x * (2.0 / math.pi) + 0.5)
    r = x - turns * 1.5703125
    r = r - turns * 4.837512969970703125e-4
    r = r - turns * 7.54978995489188216e-8
    z = r * r
    sine = r + r * z * (-1.6666654611e-1 + z * (8.3321608736e-3 - z * 1.9515295891e-4))
    cosine = 4.166664568298827e-2 + z * (-1.388731625493765e-3 + z * 2.443315711809948e-5)
    cosine = 1.0 - 0.5 * z + z * z * cosine
    quarter = turns.astype(jnp.int32)
    swap = (quarter & 1) == 1
    c = jnp.where(swap, sine, cosine)
    s = jnp.where(swap, cosine, sine)
    return jnp.where(((quarter + 1) & 2) == 2, -c, c), jnp.where((quarter & 2) == 2, -s, s)


def flag_columns(rows):
    count, width = rows.shape
    flags = jnp.concatenate([rows, jnp.zeros((WIDTH - count, width), f32)])
    if width < WIDTH:
        flags = jnp.concatenate([flags, jnp.zeros((WIDTH, WIDTH - width), f32)], 1)
    return jnp.transpose(flags)


def table_kernel(
    place,
    angles_far,
    three_far,
    four_far,
    fixed_far,
    high,
    low,
    far_cos,
    far_sin,
    flags,
    keep,
    angles,
    need_three,
    need_four,
    fixed,
    sems,
):
    copies = [
        pltpu.make_async_copy(far, near, sems.at[i])
        for i, (far, near) in enumerate(
            (
                (angles_far, angles),
                (three_far, need_three),
                (four_far, need_four),
                (fixed_far, fixed),
            )
        )
    ]
    for copy in copies:
        copy.start()
    cones, boxes = need_three.shape
    fours = need_four.shape[1]
    copies[1].wait()
    flags[...] = flag_columns(need_three[...].astype(f32))
    copies[2].wait()
    four_flags = flag_columns(need_four[...].astype(f32))
    for c in range(cones):
        keep[pl.ds(c * fours, fours), :] = jnp.broadcast_to(
            four_flags[:fours, c : c + 1], (fours, WIDTH)
        )
    copies[0].wait()
    row = lax.broadcasted_iota(jnp.int32, (8, WIDTH), 0)
    polar = jnp.zeros((8, WIDTH), f32)
    azimuth = jnp.zeros((8, WIDTH), f32)
    for c in range(cones):
        polar = jnp.where(row == c, angles[0, place[0] * cones + c], polar)
        azimuth = jnp.where(row == c, angles[1, place[0] * cones + c], azimuth)
    cos_p, sin_p = cosine_sine(polar)
    cos_a, sin_a = cosine_sine(azimuth)
    direction = (sin_p * cos_a, sin_p * sin_a, cos_p)
    real = lax.broadcasted_iota(jnp.int32, (NODES, WIDTH), 1) < NODES
    copies[3].wait()
    octants = 3 * NODES
    quarters = octants + 6 * OCTANTS
    for c in range(cones):
        along = [direction[d][c : c + 1, :] for d in range(3)]

        def dot(start, size):
            value = along[0] * fixed[start : start + size, :]
            value = value + along[1] * fixed[start + size : start + 2 * size, :]
            return value + along[2] * fixed[start + 2 * size : start + 3 * size, :]

        c0, s0 = cosine_sine(dot(0, NODES))
        even = jnp.where(real, c0, -s0)
        odd = jnp.where(real, -s0, -c0)
        c1, s1 = cosine_sine(dot(octants, OCTANTS))
        for o in range(OCTANTS):
            value = even * c1[o : o + 1, :] + odd * s1[o : o + 1, :]
            value = value * fixed[quarters + o * NODES : quarters + (o + 1) * NODES, :]
            top, rest = split(value)
            high[o * NODES : (o + 1) * NODES, c * WIDTH : (c + 1) * WIDTH] = top
            low[o * NODES : (o + 1) * NODES, c * WIDTH : (c + 1) * WIDTH] = rest
        c3, s3 = cosine_sine(dot(octants + 3 * OCTANTS, OCTANTS))
        far_cos[c * OCTANTS : (c + 1) * OCTANTS, :] = c3
        far_sin[c * OCTANTS : (c + 1) * OCTANTS, :] = jnp.where(real[:OCTANTS], s3, -s3)


def level_kernel(
    place, gathered, high, low, far_cos, far_sin, flags, keep, weights, out, lowfreq, turned
):
    lowfreq[...] = gathered[pl.ds(pl.multiple_of(place[0] * OCTANTS, OCTANTS), OCTANTS), :]
    boxes = gathered.shape[0] // OCTANTS
    rows = keep.shape[0]
    real = lax.broadcasted_iota(jnp.int32, (boxes, WIDTH), 1) < NODES
    reals, imags = [], []
    for o in range(0, OCTANTS, 2):
        a = gathered[pl.ds(o, boxes, stride=OCTANTS), :]
        b = gathered[pl.ds(o + 1, boxes, stride=OCTANTS), :]
        reals.append(jnp.where(real, a, pltpu.roll(b, NODES, 1)))
        imags.append(jnp.where(real, pltpu.roll(a, NODES, 1), b))
    both = jnp.concatenate([jnp.concatenate(reals, 1), jnp.concatenate(imags, 1)])
    top, rest = split(both)
    product = jnp.dot(jnp.concatenate([top, rest]), high[...], preferred_element_type=f32)
    product = product[: 2 * boxes] + (
        product[2 * boxes :] + jnp.dot(top, low[...], preferred_element_type=f32)
    )
    for c in range(product.shape[1] // WIDTH):
        part = product[:, c * WIDTH : (c + 1) * WIDTH]
        across = pltpu.roll(part[boxes:], NODES, 1)
        three = part[:boxes] + jnp.where(real, -across, across)
        three = three * jnp.broadcast_to(flags[:, c : c + 1], (boxes, WIDTH))
        at = slice(c * OCTANTS, (c + 1) * OCTANTS)
        cosine = jnp.concatenate([far_cos[at, :]] * (boxes // OCTANTS))
        sine = jnp.concatenate([far_sin[at, :]] * (boxes // OCTANTS))
        turned[pl.ds(c * boxes, boxes), :] = cosine * three + sine * pltpu.roll(three, NODES, 1)
    parts = [turned[pl.ds(o, rows, stride=OCTANTS), :] for o in range(OCTANTS)]
    four = times(jnp.concatenate(parts, 1), weights[...])
    out[...] = (four * keep[...]).reshape(out.shape)


def hbm():
    return pl.BlockSpec(memory_space=pltpu.HBM)


def vmem():
    return pl.BlockSpec(memory_space=pltpu.VMEM)


def smem():
    return pl.BlockSpec(memory_space=pltpu.SMEM)


def here(array):
    return pltpu.with_memory_space_constraint(array, pltpu.VMEM)


def local(leaf_expansions, leaf_occupied, cone_angles, cone_need3, cone_need4):
    rows, width = leaf_expansions.shape
    cones, boxes = cone_need3.shape
    fours = cone_need4.shape[1]
    subs = lax.axis_size("sub")
    blocks = lax.axis_size("z") * lax.axis_size("y")
    place = lax.axis_index(("half", "z", "y")).reshape(1)
    parts, doubled = transfer_rows()
    weights = jnp.asarray(parts)
    narrow = parts.reshape(OCTANTS, 2, NODES, 4, NODES)[:, 0, :, ::2].reshape(-1, width)
    partial = pl.pallas_call(
        leaf_kernel,
        out_shape=jax.ShapeDtypeStruct((subs, 8, width), f32),
        in_specs=[smem(), hbm(), hbm(), hbm()],
        out_specs=vmem(),
        scratch_shapes=[
            pltpu.VMEM((rows // width, width), jnp.int32),
            pltpu.VMEM(narrow.shape, bf16),
            pltpu.VMEM((rows, width), f32),
            pltpu.VMEM(parts.shape, bf16),
            pltpu.VMEM((rows, width), f32),
            pltpu.VMEM((rows // 8, width), f32),
            pltpu.SemaphoreType.DMA((3,)),
        ],
        compiler_params=pltpu.CompilerParams(vmem_limit_bytes=60 << 20),
        name="leaves",
    )(
        lax.axis_index("sub").reshape(1),
        leaf_occupied.reshape(rows // 128, 128),
        jnp.asarray(narrow),
        leaf_expansions,
    )
    received = lax.all_to_all(partial, "sub", split_axis=0, concat_axis=0, tiled=True)
    fixed = np.concatenate([near_columns(), octant_rows(), doubled])
    tables = pl.pallas_call(
        table_kernel,
        out_shape=[
            pltpu.VMEM((OCTANTS * NODES, cones * width), bf16),
            pltpu.VMEM((OCTANTS * NODES, cones * width), bf16),
            pltpu.VMEM((cones * OCTANTS, width), f32),
            pltpu.VMEM((cones * OCTANTS, width), f32),
            pltpu.VMEM((boxes, width), f32),
            pltpu.VMEM((cones * fours, width), f32),
        ],
        in_specs=[smem()] + [hbm()] * 4,
        out_specs=[vmem()] * 6,
        scratch_shapes=[
            pltpu.SMEM(cone_angles.shape, f32),
            pltpu.VMEM(cone_need3.shape, jnp.int32),
            pltpu.VMEM(cone_need4.shape, jnp.int32),
            pltpu.VMEM(fixed.shape, f32),
            pltpu.SemaphoreType.DMA((4,)),
        ],
        compiler_params=pltpu.CompilerParams(vmem_limit_bytes=60 << 20),
        name="tables",
    )(
        place,
        cone_angles,
        cone_need3,
        cone_need4,
        jnp.asarray(fixed),
    )
    received, *tables = lax.optimization_barrier((received, *tables))
    gathered = lax.all_to_all(
        jnp.broadcast_to(received.sum(axis=0)[None], (blocks, 8, width)),
        ("z", "y"),
        split_axis=0,
        concat_axis=0,
        tiled=True,
    )
    gathered = lax.all_gather(gathered.reshape(blocks * 8, width), "half", tiled=True)
    cone_expansions, lowfreq = pl.pallas_call(
        level_kernel,
        out_shape=[
            jax.ShapeDtypeStruct((cones, fours, width), f32),
            jax.ShapeDtypeStruct((8, width), f32),
        ],
        in_specs=[smem()] + [vmem()] * 8,
        out_specs=[vmem(), vmem()],
        scratch_shapes=[pltpu.VMEM((cones * boxes, width), f32)],
        compiler_params=pltpu.CompilerParams(vmem_limit_bytes=24 << 20),
        name="levels",
    )(place, here(gathered), *[here(table) for table in tables], weights)
    return (lowfreq, cone_expansions)


def solution(mesh):
    halves, blocks, subs = mesh.devices.shape
    fine = Mesh(
        mesh.devices.reshape(halves, blocks // OCTANTS, OCTANTS, subs), ("half", "z", "y", "sub")
    )
    blk = ("half", "z", "y")
    return jax.shard_map(
        local,
        mesh=fine,
        in_specs=(
            P(blk + ("sub",), None),
            P(blk + ("sub",)),
            P(),
            P(blk, "sub"),
            P(blk, "sub"),
        ),
        out_specs=(P(blk + ("sub",), None), P(blk, "sub", None)),
        check_vma=False,
    )
```

```python
import math

import jax
import jax.numpy as jnp
import numpy as np
from jax import lax
from jax.experimental import pallas as pl
from jax.experimental.pallas import tpu as pltpu
from jax.sharding import Mesh
from jax.sharding import PartitionSpec as P

ORDER = 4
NODES = ORDER**3
OCTANTS = 8
WIDTH = 2 * NODES
NEAR = 1.5
FAR = 3.0
f32 = jnp.float32
bf16 = jnp.bfloat16


def points():
    index = np.arange(ORDER, dtype=np.float64)
    return np.cos((2.0 * index + 1.0) * math.pi / (2.0 * ORDER))


def transfer_rows():
    here = points()
    degree = np.arange(1, ORDER)
    single = []
    for sign in (-1.0, 1.0):
        there = (here + sign) / 2.0
        poly_here = np.cos(degree[None, :] * np.arccos(here)[:, None])
        poly_there = np.cos(degree[None, :] * np.arccos(there)[:, None])
        single.append(1.0 / ORDER + 2.0 / ORDER * poly_there @ poly_here.T)
    rows, quarters = [], []
    for octant in range(OCTANTS):
        along = [single[octant // 4 % 2], single[octant // 2 % 2], single[octant % 2]]
        full = np.kron(np.kron(along[0], along[1]), along[2])
        rows.append(np.kron(np.eye(2), full))
        quarters.append(np.kron(np.ones((1, 2)), full))
    table = np.concatenate(rows).astype(np.float32)
    high = table.astype(bf16)
    low = (table - high.astype(np.float32)).astype(bf16)
    return np.concatenate([high, low], 1), np.concatenate(quarters).astype(np.float32)


def near_columns():
    here = points()
    index = np.arange(NODES)
    coords = np.stack([here[index // ORDER**2], here[index // ORDER % ORDER], here[index % ORDER]])
    return np.tile(NEAR * coords.reshape(-1, 1), (1, WIDTH)).astype(np.float32)


def octant_rows():
    here = points()
    index = np.arange(NODES)
    coords = np.stack([here[index // ORDER**2], here[index // ORDER % ORDER], here[index % ORDER]])
    coords = np.concatenate([coords, coords], 1)
    octant = np.arange(OCTANTS)
    signs = np.stack([octant // 4 % 2, octant // 2 % 2, octant % 2]) * 2.0 - 1.0
    near = np.tile(NEAR * signs[:, :, None], (1, 1, WIDTH))
    far = FAR * (coords[:, None, :] + signs[:, :, None])
    return np.concatenate([near, far]).astype(np.float32).reshape(-1, WIDTH)


def split(value):
    high = value.astype(bf16)
    low = (value - high.astype(f32)).astype(bf16)
    return high, low


def joined(product, rows):
    top = product[:rows]
    bottom = product[rows:]
    return top[:, :WIDTH] + (top[:, WIDTH:] + bottom[:, :WIDTH]) + bottom[:, WIDTH:]


def times(value, weights):
    high, low = split(value)
    product = jnp.dot(jnp.concatenate([high, low]), weights, preferred_element_type=f32)
    return joined(product, value.shape[0])


def packed(even, odd):
    real = lax.broadcasted_iota(jnp.int32, even.shape, 1) < NODES
    reals = jnp.where(real, even, pltpu.roll(odd, NODES, 1))
    imags = jnp.where(real, pltpu.roll(even, NODES, 1), odd)
    return reals, imags


def leaf_kernel(
    place,
    occupied_far,
    narrow_far,
    leaves_far,
    out,
    occupied,
    narrow,
    leaves,
    weights,
    masked,
    first,
    sems,
):
    copies = [
        pltpu.make_async_copy(far, near, sems.at[i])
        for i, (far, near) in enumerate(
            ((occupied_far, occupied), (narrow_far, narrow), (leaves_far, leaves))
        )
    ]
    for copy in copies:
        copy.start()
    rows = leaves.shape[0]
    copies[0].wait()
    columns = []
    for block in range(rows // WIDTH):
        line = occupied[block : block + 1, :].astype(f32)
        columns.append(jnp.transpose(jnp.broadcast_to(line, (WIDTH, WIDTH))))
    copies[1].wait()
    real = lax.broadcasted_iota(jnp.int32, (NODES, WIDTH), 1) < NODES
    for o in range(OCTANTS):
        value = narrow[o * NODES : (o + 1) * NODES, :].astype(f32)
        other = pltpu.roll(value, NODES, 1)
        top = pl.ds(o * WIDTH, NODES)
        bottom = pl.ds(o * WIDTH + NODES, NODES)
        weights[top, :WIDTH] = jnp.where(real, value, 0.0).astype(bf16)
        weights[top, WIDTH:] = jnp.where(real, other, 0.0).astype(bf16)
        weights[bottom, :WIDTH] = jnp.where(real, 0.0, other).astype(bf16)
        weights[bottom, WIDTH:] = jnp.where(real, 0.0, value).astype(bf16)
    copies[2].wait()
    for block in range(rows // WIDTH):
        at = pl.ds(WIDTH * block, WIDTH)
        masked[at, :] = leaves[at, :] * columns[block]
    boxes = rows // OCTANTS
    parts = [masked[pl.ds(o, boxes, stride=OCTANTS), :] for o in range(OCTANTS)]
    first[...] = times(jnp.concatenate(parts, 1), weights[...])
    pairs = [first[pl.ds(r, boxes // 2, stride=2), :] for r in range(2)]
    start = pl.multiple_of(place[0] * (2 * WIDTH), 2 * WIDTH)
    own = weights[pl.ds(start, 2 * WIDTH), :]
    second = times(jnp.concatenate(pairs, 1), own)
    count = second.shape[0]
    first[pl.ds(0, count), :] = second
    reals, imags = packed(*[first[pl.ds(i, count // 2, stride=2), :] for i in range(2)])
    for s in range(out.shape[0]):
        at = slice(s * OCTANTS // 2, (s + 1) * OCTANTS // 2)
        out[s, : OCTANTS // 2, :] = reals[at]
        out[s, OCTANTS // 2 :, :] = imags[at]


def cosine_sine(x):
    turns = jnp.floor(x * (2.0 / math.pi) + 0.5)
    r = x - turns * 1.5703125
    r = r - turns * 4.837512969970703125e-4
    r = r - turns * 7.54978995489188216e-8
    z = r * r
    sine = r + r * z * (-1.6666654611e-1 + z * (8.3321608736e-3 - z * 1.9515295891e-4))
    cosine = 4.166664568298827e-2 + z * (-1.388731625493765e-3 + z * 2.443315711809948e-5)
    cosine = 1.0 - 0.5 * z + z * z * cosine
    quarter = turns.astype(jnp.int32)
    swap = (quarter & 1) == 1
    c = jnp.where(swap, sine, cosine)
    s = jnp.where(swap, cosine, sine)
    return jnp.where(((quarter + 1) & 2) == 2, -c, c), jnp.where((quarter & 2) == 2, -s, s)


def flag_columns(rows):
    count, width = rows.shape
    flags = jnp.concatenate([rows, jnp.zeros((WIDTH - count, width), f32)])
    if width < WIDTH:
        flags = jnp.concatenate([flags, jnp.zeros((WIDTH, WIDTH - width), f32)], 1)
    return jnp.transpose(flags)


def table_kernel(
    place,
    angles_far,
    three_far,
    four_far,
    fixed_far,
    high,
    low,
    far_cos,
    far_sin,
    keep,
    angles,
    need_three,
    need_four,
    fixed,
    sems,
):
    copies = [
        pltpu.make_async_copy(far, near, sems.at[i])
        for i, (far, near) in enumerate(
            (
                (angles_far, angles),
                (three_far, need_three),
                (four_far, need_four),
                (fixed_far, fixed),
            )
        )
    ]
    for copy in copies:
        copy.start()
    cones, boxes = need_three.shape
    fours = need_four.shape[1]
    copies[1].wait()
    three_flags = flag_columns(need_three[...].astype(f32))
    copies[2].wait()
    four_flags = flag_columns(need_four[...].astype(f32))
    for c in range(cones):
        keep[pl.ds(c * fours, fours), :] = jnp.broadcast_to(
            four_flags[:fours, c : c + 1], (fours, WIDTH)
        )
    copies[0].wait()
    row = lax.broadcasted_iota(jnp.int32, (8, WIDTH), 0)
    polar = jnp.zeros((8, WIDTH), f32)
    azimuth = jnp.zeros((8, WIDTH), f32)
    for c in range(cones):
        polar = jnp.where(row == c, angles[0, place[0] * cones + c], polar)
        azimuth = jnp.where(row == c, angles[1, place[0] * cones + c], azimuth)
    cos_p, sin_p = cosine_sine(polar)
    cos_a, sin_a = cosine_sine(azimuth)
    direction = (sin_p * cos_a, sin_p * sin_a, cos_p)
    real = lax.broadcasted_iota(jnp.int32, (NODES, WIDTH), 1) < NODES
    copies[3].wait()
    octants = 3 * NODES
    quarters = octants + 6 * OCTANTS
    for c in range(cones):
        along = [direction[d][c : c + 1, :] for d in range(3)]

        def dot(start, size):
            value = along[0] * fixed[start : start + size, :]
            value = value + along[1] * fixed[start + size : start + 2 * size, :]
            return value + along[2] * fixed[start + 2 * size : start + 3 * size, :]

        c0, s0 = cosine_sine(dot(0, NODES))
        even = jnp.where(real, c0, -s0)
        odd = jnp.where(real, -s0, -c0)
        c1, s1 = cosine_sine(dot(octants, OCTANTS))
        for o in range(OCTANTS):
            value = even * c1[o : o + 1, :] + odd * s1[o : o + 1, :]
            value = value * fixed[quarters + o * NODES : quarters + (o + 1) * NODES, :]
            top, rest = split(value)
            high[o * NODES : (o + 1) * NODES, c * WIDTH : (c + 1) * WIDTH] = top
            low[o * NODES : (o + 1) * NODES, c * WIDTH : (c + 1) * WIDTH] = rest
        c3, s3 = cosine_sine(dot(octants + 3 * OCTANTS, OCTANTS))
        column = jnp.broadcast_to(three_flags[:, c : c + 1], (boxes, WIDTH))
        at = pl.ds(c * boxes, boxes)
        far_cos[at, :] = jnp.concatenate([c3] * (boxes // OCTANTS)) * column
        far_sin[at, :] = jnp.concatenate([s3] * (boxes // OCTANTS)) * column


def level_kernel(
    place, gathered, high, low, far_cos, far_sin, keep, weights, out, lowfreq, turned
):
    boxes = gathered.shape[0] // OCTANTS
    rows = keep.shape[0]
    half = OCTANTS // 2
    own = gathered[pl.ds(pl.multiple_of(place[0] * OCTANTS, OCTANTS), OCTANTS), :]
    even, odd = packed(own[:half], own[half:])
    for p in range(half):
        lowfreq[2 * p : 2 * p + 1, :] = even[p : p + 1]
        lowfreq[2 * p + 1 : 2 * p + 2, :] = odd[p : p + 1]
    both = jnp.concatenate(
        [
            jnp.concatenate(
                [gathered[pl.ds(i * half + p, boxes, stride=OCTANTS), :] for p in range(half)], 1
            )
            for i in range(2)
        ]
    )
    top, rest = split(both)
    product = jnp.dot(jnp.concatenate([top, rest]), high[...], preferred_element_type=f32)
    product = product[: 2 * boxes] + (
        product[2 * boxes :] + jnp.dot(top, low[...], preferred_element_type=f32)
    )
    real = lax.broadcasted_iota(jnp.int32, (boxes, WIDTH), 1) < NODES
    sign = jnp.where(real, 1.0, -1.0)
    for c in range(product.shape[1] // WIDTH):
        reals = product[:boxes, c * WIDTH : (c + 1) * WIDTH]
        imags = product[boxes:, c * WIDTH : (c + 1) * WIDTH]
        at = pl.ds(c * boxes, boxes)
        cosine = far_cos[at, :]
        sine = far_sin[at, :]
        across = (cosine * imags - sine * reals) * sign
        turned[at, :] = (cosine * reals + sine * imags) + pltpu.roll(across, NODES, 1)
    parts = [turned[pl.ds(o, rows, stride=OCTANTS), :] for o in range(OCTANTS)]
    four = times(jnp.concatenate(parts, 1), weights[...])
    out[...] = (four * keep[...]).reshape(out.shape)


def hbm():
    return pl.BlockSpec(memory_space=pltpu.HBM)


def vmem():
    return pl.BlockSpec(memory_space=pltpu.VMEM)


def smem():
    return pl.BlockSpec(memory_space=pltpu.SMEM)


def here(array):
    return pltpu.with_memory_space_constraint(array, pltpu.VMEM)


def local(leaf_expansions, leaf_occupied, cone_angles, cone_need3, cone_need4):
    rows, width = leaf_expansions.shape
    cones, boxes = cone_need3.shape
    fours = cone_need4.shape[1]
    subs = lax.axis_size("sub")
    blocks = lax.axis_size("z") * lax.axis_size("y")
    place = lax.axis_index(("half", "z", "y")).reshape(1)
    parts, doubled = transfer_rows()
    weights = jnp.asarray(parts)
    narrow = parts.reshape(OCTANTS, 2, NODES, 4, NODES)[:, 0, :, ::2].reshape(-1, width)
    partial = pl.pallas_call(
        leaf_kernel,
        out_shape=jax.ShapeDtypeStruct((subs, 8, width), f32),
        in_specs=[smem(), hbm(), hbm(), hbm()],
        out_specs=vmem(),
        scratch_shapes=[
            pltpu.VMEM((rows // width, width), jnp.int32),
            pltpu.VMEM(narrow.shape, bf16),
            pltpu.VMEM((rows, width), f32),
            pltpu.VMEM(parts.shape, bf16),
            pltpu.VMEM((rows, width), f32),
            pltpu.VMEM((rows // 8, width), f32),
            pltpu.SemaphoreType.DMA((3,)),
        ],
        compiler_params=pltpu.CompilerParams(vmem_limit_bytes=60 << 20),
        name="leaves",
    )(
        lax.axis_index("sub").reshape(1),
        leaf_occupied.reshape(rows // 128, 128),
        jnp.asarray(narrow),
        leaf_expansions,
    )
    received = lax.all_to_all(partial, "sub", split_axis=0, concat_axis=0, tiled=True)
    fixed = np.concatenate([near_columns(), octant_rows(), doubled])
    tables = pl.pallas_call(
        table_kernel,
        out_shape=[
            pltpu.VMEM((OCTANTS * NODES, cones * width), bf16),
            pltpu.VMEM((OCTANTS * NODES, cones * width), bf16),
            pltpu.VMEM((cones * boxes, width), f32),
            pltpu.VMEM((cones * boxes, width), f32),
            pltpu.VMEM((cones * fours, width), f32),
        ],
        in_specs=[smem()] + [hbm()] * 4,
        out_specs=[vmem()] * 5,
        scratch_shapes=[
            pltpu.SMEM(cone_angles.shape, f32),
            pltpu.VMEM(cone_need3.shape, jnp.int32),
            pltpu.VMEM(cone_need4.shape, jnp.int32),
            pltpu.VMEM(fixed.shape, f32),
            pltpu.SemaphoreType.DMA((4,)),
        ],
        compiler_params=pltpu.CompilerParams(vmem_limit_bytes=60 << 20),
        name="tables",
    )(
        place,
        cone_angles,
        cone_need3,
        cone_need4,
        jnp.asarray(fixed),
    )
    received, *tables = lax.optimization_barrier((received, *tables))
    gathered = lax.all_to_all(
        jnp.broadcast_to(received.sum(axis=0)[None], (blocks, 8, width)),
        ("z", "y"),
        split_axis=0,
        concat_axis=0,
        tiled=True,
    )
    gathered = lax.all_gather(gathered.reshape(blocks * 8, width), "half", tiled=True)
    cone_expansions, lowfreq = pl.pallas_call(
        level_kernel,
        out_shape=[
            jax.ShapeDtypeStruct((cones, fours, width), f32),
            jax.ShapeDtypeStruct((8, width), f32),
        ],
        in_specs=[smem()] + [vmem()] * 7,
        out_specs=[vmem(), vmem()],
        scratch_shapes=[pltpu.VMEM((cones * boxes, width), f32)],
        compiler_params=pltpu.CompilerParams(vmem_limit_bytes=24 << 20),
        name="levels",
    )(place, here(gathered), *[here(table) for table in tables], weights)
    return (lowfreq, cone_expansions)


def solution(mesh):
    halves, blocks, subs = mesh.devices.shape
    fine = Mesh(
        mesh.devices.reshape(halves, blocks // OCTANTS, OCTANTS, subs), ("half", "z", "y", "sub")
    )
    blk = ("half", "z", "y")
    return jax.shard_map(
        local,
        mesh=fine,
        in_specs=(
            P(blk + ("sub",), None),
            P(blk + ("sub",)),
            P(),
            P(blk, "sub"),
            P(blk, "sub"),
        ),
        out_specs=(P(blk + ("sub",), None), P(blk, "sub", None)),
        check_vma=False,
    )
```

```python
import math

import jax
import jax.numpy as jnp
import numpy as np
from jax import lax
from jax.experimental import pallas as pl
from jax.experimental.pallas import tpu as pltpu
from jax.sharding import Mesh
from jax.sharding import PartitionSpec as P

ORDER = 4
NODES = ORDER**3
OCTANTS = 8
WIDTH = 2 * NODES
NEAR = 1.5
FAR = 3.0
f32 = jnp.float32
bf16 = jnp.bfloat16


def points():
    index = np.arange(ORDER, dtype=np.float64)
    return np.cos((2.0 * index + 1.0) * math.pi / (2.0 * ORDER))


def transfer_rows():
    here = points()
    degree = np.arange(1, ORDER)
    single = []
    for sign in (-1.0, 1.0):
        there = (here + sign) / 2.0
        poly_here = np.cos(degree[None, :] * np.arccos(here)[:, None])
        poly_there = np.cos(degree[None, :] * np.arccos(there)[:, None])
        single.append(1.0 / ORDER + 2.0 / ORDER * poly_there @ poly_here.T)
    rows, quarters = [], []
    for octant in range(OCTANTS):
        along = [single[octant // 4 % 2], single[octant // 2 % 2], single[octant % 2]]
        full = np.kron(np.kron(along[0], along[1]), along[2])
        rows.append(np.kron(np.eye(2), full))
        quarters.append(np.kron(np.ones((1, 2)), full))
    table = np.concatenate(rows).astype(np.float32)
    high = table.astype(bf16)
    low = (table - high.astype(np.float32)).astype(bf16)
    return np.concatenate([high, low], 1), np.concatenate(quarters).astype(np.float32)


def near_columns():
    here = points()
    index = np.arange(NODES)
    coords = np.stack([here[index // ORDER**2], here[index // ORDER % ORDER], here[index % ORDER]])
    return np.tile(NEAR * coords.reshape(-1, 1), (1, WIDTH)).astype(np.float32)


def octant_rows():
    here = points()
    index = np.arange(NODES)
    coords = np.stack([here[index // ORDER**2], here[index // ORDER % ORDER], here[index % ORDER]])
    coords = np.concatenate([coords, coords], 1)
    octant = np.arange(OCTANTS)
    signs = np.stack([octant // 4 % 2, octant // 2 % 2, octant % 2]) * 2.0 - 1.0
    near = np.tile(NEAR * signs[:, :, None], (1, 1, WIDTH))
    far = FAR * (coords[:, None, :] + signs[:, :, None])
    return np.concatenate([near, far]).astype(np.float32).reshape(-1, WIDTH)


def split(value):
    high = value.astype(bf16)
    low = (value - high.astype(f32)).astype(bf16)
    return high, low


def joined(product, rows):
    top = product[:rows]
    bottom = product[rows:]
    return top[:, :WIDTH] + (top[:, WIDTH:] + bottom[:, :WIDTH]) + bottom[:, WIDTH:]


def times(value, weights):
    high, low = split(value)
    product = jnp.dot(jnp.concatenate([high, low]), weights, preferred_element_type=f32)
    return joined(product, value.shape[0])


def packed(even, odd):
    real = lax.broadcasted_iota(jnp.int32, even.shape, 1) < NODES
    reals = jnp.where(real, even, pltpu.roll(odd, NODES, 1))
    imags = jnp.where(real, pltpu.roll(even, NODES, 1), odd)
    return reals, imags


def leaf_kernel(
    occupied_far,
    narrow_far,
    leaves_far,
    out,
    occupied,
    narrow,
    leaves,
    weights,
    masked,
    first,
    sems,
):
    copies = [
        pltpu.make_async_copy(far, near, sems.at[i])
        for i, (far, near) in enumerate(
            ((occupied_far, occupied), (narrow_far, narrow), (leaves_far, leaves))
        )
    ]
    for copy in copies:
        copy.start()
    rows = leaves.shape[0]
    copies[0].wait()
    columns = []
    for block in range(rows // WIDTH):
        line = occupied[block : block + 1, :].astype(f32)
        columns.append(jnp.transpose(jnp.broadcast_to(line, (WIDTH, WIDTH))))
    copies[1].wait()
    real = lax.broadcasted_iota(jnp.int32, (NODES, WIDTH), 1) < NODES
    for o in range(OCTANTS):
        value = narrow[o * NODES : (o + 1) * NODES, :].astype(f32)
        other = pltpu.roll(value, NODES, 1)
        top = pl.ds(o * WIDTH, NODES)
        bottom = pl.ds(o * WIDTH + NODES, NODES)
        weights[top, :WIDTH] = jnp.where(real, value, 0.0).astype(bf16)
        weights[top, WIDTH:] = jnp.where(real, other, 0.0).astype(bf16)
        weights[bottom, :WIDTH] = jnp.where(real, 0.0, other).astype(bf16)
        weights[bottom, WIDTH:] = jnp.where(real, 0.0, value).astype(bf16)
    copies[2].wait()
    for block in range(rows // WIDTH):
        at = pl.ds(WIDTH * block, WIDTH)
        masked[at, :] = leaves[at, :] * columns[block]
    boxes = rows // OCTANTS
    parts = [masked[pl.ds(o, boxes, stride=OCTANTS), :] for o in range(OCTANTS)]
    first[...] = times(jnp.concatenate(parts, 1), weights[...])
    pairs = [first[pl.ds(r, boxes // 2, stride=2), :] for r in range(2)]
    start = pl.multiple_of(lax.axis_index("sub") * (2 * WIDTH), 2 * WIDTH)
    own = weights[pl.ds(start, 2 * WIDTH), :]
    second = times(jnp.concatenate(pairs, 1), own)
    count = second.shape[0]
    first[pl.ds(0, count), :] = second
    reals, imags = packed(*[first[pl.ds(i, count // 2, stride=2), :] for i in range(2)])
    for s in range(out.shape[0]):
        at = slice(s * OCTANTS // 2, (s + 1) * OCTANTS // 2)
        out[s, : OCTANTS // 2, :] = reals[at]
        out[s, OCTANTS // 2 :, :] = imags[at]


def cosine_sine(x):
    turns = jnp.floor(x * (2.0 / math.pi) + 0.5)
    r = x - turns * 1.5703125
    r = r - turns * 4.837512969970703125e-4
    r = r - turns * 7.54978995489188216e-8
    z = r * r
    sine = r + r * z * (-1.6666654611e-1 + z * (8.3321608736e-3 - z * 1.9515295891e-4))
    cosine = 4.166664568298827e-2 + z * (-1.388731625493765e-3 + z * 2.443315711809948e-5)
    cosine = 1.0 - 0.5 * z + z * z * cosine
    quarter = turns.astype(jnp.int32)
    swap = (quarter & 1) == 1
    c = jnp.where(swap, sine, cosine)
    s = jnp.where(swap, cosine, sine)
    return jnp.where(((quarter + 1) & 2) == 2, -c, c), jnp.where((quarter & 2) == 2, -s, s)


def flag_columns(rows):
    count, width = rows.shape
    flags = jnp.concatenate([rows, jnp.zeros((WIDTH - count, width), f32)])
    if width < WIDTH:
        flags = jnp.concatenate([flags, jnp.zeros((WIDTH, WIDTH - width), f32)], 1)
    return jnp.transpose(flags)


def table_kernel(
    angles_far,
    three_far,
    four_far,
    fixed_far,
    high,
    low,
    far_cos,
    far_sin,
    keep,
    angles,
    need_three,
    need_four,
    fixed,
    sems,
):
    copies = [
        pltpu.make_async_copy(far, near, sems.at[i])
        for i, (far, near) in enumerate(
            (
                (angles_far, angles),
                (three_far, need_three),
                (four_far, need_four),
                (fixed_far, fixed),
            )
        )
    ]
    for copy in copies:
        copy.start()
    cones, boxes = need_three.shape
    fours = need_four.shape[1]
    copies[1].wait()
    three_flags = flag_columns(need_three[...].astype(f32))
    copies[2].wait()
    four_flags = flag_columns(need_four[...].astype(f32))
    for c in range(cones):
        keep[pl.ds(c * fours, fours), :] = jnp.broadcast_to(
            four_flags[:fours, c : c + 1], (fours, WIDTH)
        )
    copies[0].wait()
    row = lax.broadcasted_iota(jnp.int32, (8, WIDTH), 0)
    start = lax.axis_index(("half", "z", "y")) * cones
    polar = jnp.zeros((8, WIDTH), f32)
    azimuth = jnp.zeros((8, WIDTH), f32)
    for c in range(cones):
        polar = jnp.where(row == c, angles[0, start + c], polar)
        azimuth = jnp.where(row == c, angles[1, start + c], azimuth)
    cos_p, sin_p = cosine_sine(polar)
    cos_a, sin_a = cosine_sine(azimuth)
    direction = (sin_p * cos_a, sin_p * sin_a, cos_p)
    real = lax.broadcasted_iota(jnp.int32, (NODES, WIDTH), 1) < NODES
    copies[3].wait()
    octants = 3 * NODES
    quarters = octants + 6 * OCTANTS
    for c in range(cones):
        along = [direction[d][c : c + 1, :] for d in range(3)]

        def dot(start, size):
            value = along[0] * fixed[start : start + size, :]
            value = value + along[1] * fixed[start + size : start + 2 * size, :]
            return value + along[2] * fixed[start + 2 * size : start + 3 * size, :]

        c0, s0 = cosine_sine(dot(0, NODES))
        even = jnp.where(real, c0, -s0)
        odd = jnp.where(real, -s0, -c0)
        c1, s1 = cosine_sine(dot(octants, OCTANTS))
        for o in range(OCTANTS):
            value = even * c1[o : o + 1, :] + odd * s1[o : o + 1, :]
            value = value * fixed[quarters + o * NODES : quarters + (o + 1) * NODES, :]
            top, rest = split(value)
            high[o * NODES : (o + 1) * NODES, c * WIDTH : (c + 1) * WIDTH] = top
            low[o * NODES : (o + 1) * NODES, c * WIDTH : (c + 1) * WIDTH] = rest
        c3, s3 = cosine_sine(dot(octants + 3 * OCTANTS, OCTANTS))
        column = jnp.broadcast_to(three_flags[:, c : c + 1], (boxes, WIDTH))
        at = pl.ds(c * boxes, boxes)
        far_cos[at, :] = jnp.concatenate([c3] * (boxes // OCTANTS)) * column
        far_sin[at, :] = jnp.concatenate([s3] * (boxes // OCTANTS)) * column


def level_kernel(
    gathered, high, low, far_cos, far_sin, keep, weights, out, lowfreq, turned
):
    boxes = gathered.shape[0] // OCTANTS
    rows = keep.shape[0]
    half = OCTANTS // 2
    start = pl.multiple_of(lax.axis_index(("half", "z", "y")) * OCTANTS, OCTANTS)
    own = gathered[pl.ds(start, OCTANTS), :]
    even, odd = packed(own[:half], own[half:])
    for p in range(half):
        lowfreq[2 * p : 2 * p + 1, :] = even[p : p + 1]
        lowfreq[2 * p + 1 : 2 * p + 2, :] = odd[p : p + 1]
    both = jnp.concatenate(
        [
            jnp.concatenate(
                [gathered[pl.ds(i * half + p, boxes, stride=OCTANTS), :] for p in range(half)], 1
            )
            for i in range(2)
        ]
    )
    top, rest = split(both)
    product = jnp.dot(jnp.concatenate([top, rest]), high[...], preferred_element_type=f32)
    product = product[: 2 * boxes] + (
        product[2 * boxes :] + jnp.dot(top, low[...], preferred_element_type=f32)
    )
    real = lax.broadcasted_iota(jnp.int32, (boxes, WIDTH), 1) < NODES
    sign = jnp.where(real, 1.0, -1.0)
    for c in range(product.shape[1] // WIDTH):
        reals = product[:boxes, c * WIDTH : (c + 1) * WIDTH]
        imags = product[boxes:, c * WIDTH : (c + 1) * WIDTH]
        at = pl.ds(c * boxes, boxes)
        cosine = far_cos[at, :]
        sine = far_sin[at, :]
        across = (cosine * imags - sine * reals) * sign
        turned[at, :] = (cosine * reals + sine * imags) + pltpu.roll(across, NODES, 1)
    parts = [turned[pl.ds(o, rows, stride=OCTANTS), :] for o in range(OCTANTS)]
    four = times(jnp.concatenate(parts, 1), weights[...])
    out[...] = (four * keep[...]).reshape(out.shape)


def hbm():
    return pl.BlockSpec(memory_space=pltpu.HBM)


def vmem():
    return pl.BlockSpec(memory_space=pltpu.VMEM)


def here(array):
    return pltpu.with_memory_space_constraint(array, pltpu.VMEM)


def local(leaf_expansions, leaf_occupied, cone_angles, cone_need3, cone_need4):
    rows, width = leaf_expansions.shape
    cones, boxes = cone_need3.shape
    fours = cone_need4.shape[1]
    subs = lax.axis_size("sub")
    blocks = lax.axis_size("z") * lax.axis_size("y")
    parts, doubled = transfer_rows()
    weights = jnp.asarray(parts)
    narrow = parts.reshape(OCTANTS, 2, NODES, 4, NODES)[:, 0, :, ::2].reshape(-1, width)
    partial = pl.pallas_call(
        leaf_kernel,
        out_shape=jax.ShapeDtypeStruct((subs, 8, width), f32),
        in_specs=[hbm()] * 3,
        out_specs=vmem(),
        scratch_shapes=[
            pltpu.VMEM((rows // width, width), jnp.int32),
            pltpu.VMEM(narrow.shape, bf16),
            pltpu.VMEM((rows, width), f32),
            pltpu.VMEM(parts.shape, bf16),
            pltpu.VMEM((rows, width), f32),
            pltpu.VMEM((rows // 8, width), f32),
            pltpu.SemaphoreType.DMA((3,)),
        ],
        compiler_params=pltpu.CompilerParams(vmem_limit_bytes=60 << 20),
        name="leaves",
    )(
        leaf_occupied.reshape(rows // 128, 128),
        jnp.asarray(narrow),
        leaf_expansions,
    )
    received = lax.all_to_all(partial, "sub", split_axis=0, concat_axis=0, tiled=True)
    fixed = np.concatenate([near_columns(), octant_rows(), doubled])
    tables = pl.pallas_call(
        table_kernel,
        out_shape=[
            pltpu.VMEM((OCTANTS * NODES, cones * width), bf16),
            pltpu.VMEM((OCTANTS * NODES, cones * width), bf16),
            pltpu.VMEM((cones * boxes, width), f32),
            pltpu.VMEM((cones * boxes, width), f32),
            pltpu.VMEM((cones * fours, width), f32),
        ],
        in_specs=[hbm()] * 4,
        out_specs=[vmem()] * 5,
        scratch_shapes=[
            pltpu.SMEM(cone_angles.shape, f32),
            pltpu.VMEM(cone_need3.shape, jnp.int32),
            pltpu.VMEM(cone_need4.shape, jnp.int32),
            pltpu.VMEM(fixed.shape, f32),
            pltpu.SemaphoreType.DMA((4,)),
        ],
        compiler_params=pltpu.CompilerParams(vmem_limit_bytes=60 << 20),
        name="tables",
    )(
        cone_angles,
        cone_need3,
        cone_need4,
        jnp.asarray(fixed),
    )
    received, *tables = lax.optimization_barrier((received, *tables))
    gathered = lax.all_to_all(
        jnp.broadcast_to(received.sum(axis=0)[None], (blocks, 8, width)),
        ("z", "y"),
        split_axis=0,
        concat_axis=0,
        tiled=True,
    )
    gathered = lax.all_gather(gathered.reshape(blocks * 8, width), "half", tiled=True)
    cone_expansions, lowfreq = pl.pallas_call(
        level_kernel,
        out_shape=[
            jax.ShapeDtypeStruct((cones, fours, width), f32),
            jax.ShapeDtypeStruct((8, width), f32),
        ],
        in_specs=[vmem()] * 7,
        out_specs=[vmem(), vmem()],
        scratch_shapes=[pltpu.VMEM((cones * boxes, width), f32)],
        compiler_params=pltpu.CompilerParams(vmem_limit_bytes=24 << 20),
        name="levels",
    )(here(gathered), *[here(table) for table in tables], weights)
    return (lowfreq, cone_expansions)


def solution(mesh):
    halves, blocks, subs = mesh.devices.shape
    fine = Mesh(
        mesh.devices.reshape(halves, blocks // OCTANTS, OCTANTS, subs), ("half", "z", "y", "sub")
    )
    blk = ("half", "z", "y")
    return jax.shard_map(
        local,
        mesh=fine,
        in_specs=(
            P(blk + ("sub",), None),
            P(blk + ("sub",)),
            P(),
            P(blk, "sub"),
            P(blk, "sub"),
        ),
        out_specs=(P(blk + ("sub",), None), P(blk, "sub", None)),
        check_vma=False,
    )
```

```python
import math

import jax
import jax.numpy as jnp
import numpy as np
from jax import lax
from jax.experimental import pallas as pl
from jax.experimental.pallas import tpu as pltpu
from jax.sharding import Mesh
from jax.sharding import PartitionSpec as P

ORDER = 4
NODES = ORDER**3
OCTANTS = 8
WIDTH = 2 * NODES
NEAR = 1.5
FAR = 3.0
f32 = jnp.float32
bf16 = jnp.bfloat16


def points():
    index = np.arange(ORDER, dtype=np.float64)
    return np.cos((2.0 * index + 1.0) * math.pi / (2.0 * ORDER))


def transfer_rows():
    here = points()
    degree = np.arange(1, ORDER)
    single = []
    for sign in (-1.0, 1.0):
        there = (here + sign) / 2.0
        poly_here = np.cos(degree[None, :] * np.arccos(here)[:, None])
        poly_there = np.cos(degree[None, :] * np.arccos(there)[:, None])
        single.append(1.0 / ORDER + 2.0 / ORDER * poly_there @ poly_here.T)
    rows, quarters = [], []
    for octant in range(OCTANTS):
        along = [single[octant // 4 % 2], single[octant // 2 % 2], single[octant % 2]]
        full = np.kron(np.kron(along[0], along[1]), along[2])
        rows.append(np.kron(np.eye(2), full))
        quarters.append(np.kron(np.ones((1, 2)), full))
    table = np.concatenate(rows).astype(np.float32)
    high = table.astype(bf16)
    low = (table - high.astype(np.float32)).astype(bf16)
    return np.concatenate([high, low], 1), np.concatenate(quarters).astype(np.float32)


def near_columns():
    here = points()
    index = np.arange(NODES)
    coords = np.stack([here[index // ORDER**2], here[index // ORDER % ORDER], here[index % ORDER]])
    return np.tile(NEAR * coords.reshape(-1, 1), (1, WIDTH)).astype(np.float32)


def octant_rows():
    here = points()
    index = np.arange(NODES)
    coords = np.stack([here[index // ORDER**2], here[index // ORDER % ORDER], here[index % ORDER]])
    coords = np.concatenate([coords, coords], 1)
    octant = np.arange(OCTANTS)
    signs = np.stack([octant // 4 % 2, octant // 2 % 2, octant % 2]) * 2.0 - 1.0
    near = np.tile(NEAR * signs[:, :, None], (1, 1, WIDTH))
    far = FAR * (coords[:, None, :] + signs[:, :, None])
    return np.concatenate([near, far]).astype(np.float32).reshape(-1, WIDTH)


def split(value):
    high = value.astype(bf16)
    low = (value - high.astype(f32)).astype(bf16)
    return high, low


def joined(product, rows):
    top = product[:rows]
    bottom = product[rows:]
    return top[:, :WIDTH] + (top[:, WIDTH:] + bottom[:, :WIDTH]) + bottom[:, WIDTH:]


def times(value, weights):
    high, low = split(value)
    product = jnp.dot(jnp.concatenate([high, low]), weights, preferred_element_type=f32)
    return joined(product, value.shape[0])


def packed(even, odd):
    real = lax.broadcasted_iota(jnp.int32, even.shape, 1) < NODES
    reals = jnp.where(real, even, pltpu.roll(odd, NODES, 1))
    imags = jnp.where(real, pltpu.roll(even, NODES, 1), odd)
    return reals, imags


def leaf_kernel(
    occupied_far,
    narrow_far,
    leaves_far,
    out,
    occupied,
    narrow,
    leaves,
    weights,
    masked,
    first,
    sems,
):
    copies = [
        pltpu.make_async_copy(far, near, sems.at[i])
        for i, (far, near) in enumerate(
            ((occupied_far, occupied), (narrow_far, narrow), (leaves_far, leaves))
        )
    ]
    for copy in copies:
        copy.start()
    rows = leaves.shape[0]
    copies[0].wait()
    columns = []
    for block in range(rows // WIDTH):
        line = occupied[block : block + 1, :].astype(f32)
        columns.append(jnp.transpose(jnp.broadcast_to(line, (WIDTH, WIDTH))))
    copies[1].wait()
    real = lax.broadcasted_iota(jnp.int32, (NODES, WIDTH), 1) < NODES
    for o in range(OCTANTS):
        value = narrow[o * NODES : (o + 1) * NODES, :].astype(f32)
        other = pltpu.roll(value, NODES, 1)
        top = pl.ds(o * WIDTH, NODES)
        bottom = pl.ds(o * WIDTH + NODES, NODES)
        weights[top, :WIDTH] = jnp.where(real, value, 0.0).astype(bf16)
        weights[top, WIDTH:] = jnp.where(real, other, 0.0).astype(bf16)
        weights[bottom, :WIDTH] = jnp.where(real, 0.0, other).astype(bf16)
        weights[bottom, WIDTH:] = jnp.where(real, 0.0, value).astype(bf16)
    copies[2].wait()
    for block in range(rows // WIDTH):
        at = pl.ds(WIDTH * block, WIDTH)
        masked[at, :] = leaves[at, :] * columns[block]
    boxes = rows // OCTANTS
    parts = [masked[pl.ds(o, boxes, stride=OCTANTS), :] for o in range(OCTANTS)]
    first[...] = times(jnp.concatenate(parts, 1), weights[...])
    pairs = [first[pl.ds(r, boxes // 2, stride=2), :] for r in range(2)]
    start = pl.multiple_of(lax.axis_index("sub") * (2 * WIDTH), 2 * WIDTH)
    own = weights[pl.ds(start, 2 * WIDTH), :]
    second = times(jnp.concatenate(pairs, 1), own)
    count = second.shape[0]
    first[pl.ds(0, count), :] = second
    reals, imags = packed(*[first[pl.ds(i, count // 2, stride=2), :] for i in range(2)])
    for s in range(out.shape[0]):
        at = slice(s * OCTANTS // 2, (s + 1) * OCTANTS // 2)
        out[s, : OCTANTS // 2, :] = reals[at]
        out[s, OCTANTS // 2 :, :] = imags[at]


def cosine_sine(x):
    turns = jnp.floor(x * (2.0 / math.pi) + 0.5)
    r = x - turns * 1.5703125
    r = r - turns * 4.837512969970703125e-4
    r = r - turns * 7.54978995489188216e-8
    z = r * r
    sine = r + r * z * (-1.6666654611e-1 + z * (8.3321608736e-3 - z * 1.9515295891e-4))
    cosine = 4.166664568298827e-2 + z * (-1.388731625493765e-3 + z * 2.443315711809948e-5)
    cosine = 1.0 - 0.5 * z + z * z * cosine
    quarter = turns.astype(jnp.int32)
    swap = (quarter & 1) == 1
    c = jnp.where(swap, sine, cosine)
    s = jnp.where(swap, cosine, sine)
    return jnp.where(((quarter + 1) & 2) == 2, -c, c), jnp.where((quarter & 2) == 2, -s, s)


def flag_columns(rows):
    count, width = rows.shape
    flags = jnp.concatenate([rows, jnp.zeros((WIDTH - count, width), f32)])
    if width < WIDTH:
        flags = jnp.concatenate([flags, jnp.zeros((WIDTH, WIDTH - width), f32)], 1)
    return jnp.transpose(flags)


def by_octant(rows, boxes):
    share = boxes // OCTANTS
    return jnp.concatenate(
        [jnp.broadcast_to(rows[o : o + 1], (share, WIDTH)) for o in range(OCTANTS)]
    )


def table_kernel(
    angles_far,
    three_far,
    four_far,
    fixed_far,
    high,
    low,
    far_cos,
    far_sin,
    keep,
    angles,
    need_three,
    need_four,
    fixed,
    flags,
    sems,
):
    copies = [
        pltpu.make_async_copy(far, near, sems.at[i])
        for i, (far, near) in enumerate(
            (
                (angles_far, angles),
                (three_far, need_three),
                (four_far, need_four),
                (fixed_far, fixed),
            )
        )
    ]
    for copy in copies:
        copy.start()
    cones, boxes = need_three.shape
    fours = need_four.shape[1]
    copies[1].wait()
    flags[...] = flag_columns(need_three[...].astype(f32))
    three_flags = jnp.concatenate(
        [flags[pl.ds(o, boxes // OCTANTS, stride=OCTANTS), :] for o in range(OCTANTS)]
    )
    copies[2].wait()
    four_flags = flag_columns(need_four[...].astype(f32))
    for c in range(cones):
        keep[pl.ds(c * fours, fours), :] = jnp.broadcast_to(
            four_flags[:fours, c : c + 1], (fours, WIDTH)
        )
    copies[0].wait()
    row = lax.broadcasted_iota(jnp.int32, (8, WIDTH), 0)
    start = lax.axis_index(("half", "z", "y")) * cones
    polar = jnp.zeros((8, WIDTH), f32)
    azimuth = jnp.zeros((8, WIDTH), f32)
    for c in range(cones):
        polar = jnp.where(row == c, angles[0, start + c], polar)
        azimuth = jnp.where(row == c, angles[1, start + c], azimuth)
    cos_p, sin_p = cosine_sine(polar)
    cos_a, sin_a = cosine_sine(azimuth)
    direction = (sin_p * cos_a, sin_p * sin_a, cos_p)
    real = lax.broadcasted_iota(jnp.int32, (NODES, WIDTH), 1) < NODES
    copies[3].wait()
    octants = 3 * NODES
    quarters = octants + 6 * OCTANTS
    for c in range(cones):
        along = [direction[d][c : c + 1, :] for d in range(3)]

        def dot(start, size):
            value = along[0] * fixed[start : start + size, :]
            value = value + along[1] * fixed[start + size : start + 2 * size, :]
            return value + along[2] * fixed[start + 2 * size : start + 3 * size, :]

        c0, s0 = cosine_sine(dot(0, NODES))
        even = jnp.where(real, c0, -s0)
        odd = jnp.where(real, -s0, -c0)
        c1, s1 = cosine_sine(dot(octants, OCTANTS))
        for o in range(OCTANTS):
            value = even * c1[o : o + 1, :] + odd * s1[o : o + 1, :]
            value = value * fixed[quarters + o * NODES : quarters + (o + 1) * NODES, :]
            top, rest = split(value)
            high[o * NODES : (o + 1) * NODES, c * WIDTH : (c + 1) * WIDTH] = top
            low[o * NODES : (o + 1) * NODES, c * WIDTH : (c + 1) * WIDTH] = rest
        c3, s3 = cosine_sine(dot(octants + 3 * OCTANTS, OCTANTS))
        column = jnp.broadcast_to(three_flags[:, c : c + 1], (boxes, WIDTH))
        at = pl.ds(c * boxes, boxes)
        far_cos[at, :] = by_octant(c3, boxes) * column
        far_sin[at, :] = by_octant(s3, boxes) * column


def level_kernel(
    gathered, high, low, far_cos, far_sin, keep, weights, out, lowfreq
):
    boxes = gathered.shape[0] // OCTANTS
    half = OCTANTS // 2
    start = pl.multiple_of(lax.axis_index(("half", "y", "z")) * OCTANTS, OCTANTS)
    own = gathered[pl.ds(start, OCTANTS), :]
    even, odd = packed(own[:half], own[half:])
    for p in range(half):
        lowfreq[2 * p : 2 * p + 1, :] = even[p : p + 1]
        lowfreq[2 * p + 1 : 2 * p + 2, :] = odd[p : p + 1]
    halves = 2
    run = boxes // halves // OCTANTS

    def octant_rows_of(row):
        starts = [
            (h * OCTANTS + o) * run * OCTANTS + row for o in range(OCTANTS) for h in range(halves)
        ]
        return jnp.concatenate([gathered[pl.ds(s, run, stride=OCTANTS), :] for s in starts])

    both = jnp.concatenate(
        [
            jnp.concatenate([octant_rows_of(i * half + p) for p in range(half)], 1)
            for i in range(2)
        ]
    )
    top, rest = split(both)
    product = jnp.dot(jnp.concatenate([top, rest]), high[...], preferred_element_type=f32)
    product = product[: 2 * boxes] + (
        product[2 * boxes :] + jnp.dot(top, low[...], preferred_element_type=f32)
    )
    real = lax.broadcasted_iota(jnp.int32, (boxes, WIDTH), 1) < NODES
    sign = jnp.where(real, 1.0, -1.0)
    cones = []
    for c in range(product.shape[1] // WIDTH):
        reals = product[:boxes, c * WIDTH : (c + 1) * WIDTH]
        imags = product[boxes:, c * WIDTH : (c + 1) * WIDTH]
        at = pl.ds(c * boxes, boxes)
        cosine = far_cos[at, :]
        sine = far_sin[at, :]
        across = (cosine * imags - sine * reals) * sign
        turned = (cosine * reals + sine * imags) + pltpu.roll(across, NODES, 1)
        share = boxes // OCTANTS
        cones.append(
            jnp.concatenate([turned[o * share : (o + 1) * share] for o in range(OCTANTS)], 1)
        )
    four = times(jnp.concatenate(cones), weights[...])
    out[...] = (four * keep[...]).reshape(out.shape)


def hbm():
    return pl.BlockSpec(memory_space=pltpu.HBM)


def vmem():
    return pl.BlockSpec(memory_space=pltpu.VMEM)


def here(array):
    return pltpu.with_memory_space_constraint(array, pltpu.VMEM)


def local(leaf_expansions, leaf_occupied, cone_angles, cone_need3, cone_need4):
    rows, width = leaf_expansions.shape
    cones, boxes = cone_need3.shape
    fours = cone_need4.shape[1]
    subs = lax.axis_size("sub")
    blocks = lax.axis_size("z") * lax.axis_size("y")
    parts, doubled = transfer_rows()
    weights = jnp.asarray(parts)
    narrow = parts.reshape(OCTANTS, 2, NODES, 4, NODES)[:, 0, :, ::2].reshape(-1, width)
    partial = pl.pallas_call(
        leaf_kernel,
        out_shape=jax.ShapeDtypeStruct((subs, 8, width), f32),
        in_specs=[hbm()] * 3,
        out_specs=vmem(),
        scratch_shapes=[
            pltpu.VMEM((rows // width, width), jnp.int32),
            pltpu.VMEM(narrow.shape, bf16),
            pltpu.VMEM((rows, width), f32),
            pltpu.VMEM(parts.shape, bf16),
            pltpu.VMEM((rows, width), f32),
            pltpu.VMEM((rows // 8, width), f32),
            pltpu.SemaphoreType.DMA((3,)),
        ],
        compiler_params=pltpu.CompilerParams(vmem_limit_bytes=60 << 20),
        name="leaves",
    )(
        leaf_occupied.reshape(rows // 128, 128),
        jnp.asarray(narrow),
        leaf_expansions,
    )
    received = lax.all_to_all(partial, "sub", split_axis=0, concat_axis=0, tiled=True)
    fixed = np.concatenate([near_columns(), octant_rows(), doubled])
    tables = pl.pallas_call(
        table_kernel,
        out_shape=[
            pltpu.VMEM((OCTANTS * NODES, cones * width), bf16),
            pltpu.VMEM((OCTANTS * NODES, cones * width), bf16),
            pltpu.VMEM((cones * boxes, width), f32),
            pltpu.VMEM((cones * boxes, width), f32),
            pltpu.VMEM((cones * fours, width), f32),
        ],
        in_specs=[hbm()] * 4,
        out_specs=[vmem()] * 5,
        scratch_shapes=[
            pltpu.SMEM(cone_angles.shape, f32),
            pltpu.VMEM(cone_need3.shape, jnp.int32),
            pltpu.VMEM(cone_need4.shape, jnp.int32),
            pltpu.VMEM(fixed.shape, f32),
            pltpu.VMEM((boxes, width), f32),
            pltpu.SemaphoreType.DMA((4,)),
        ],
        compiler_params=pltpu.CompilerParams(vmem_limit_bytes=60 << 20),
        name="tables",
    )(
        cone_angles,
        cone_need3,
        cone_need4,
        jnp.asarray(fixed),
    )
    received, *tables = lax.optimization_barrier((received, *tables))
    gathered = lax.all_to_all(
        jnp.broadcast_to(received.sum(axis=0)[None], (blocks, 8, width)),
        ("y", "z"),
        split_axis=0,
        concat_axis=0,
        tiled=True,
    )
    gathered = lax.all_gather(gathered.reshape(blocks * 8, width), "half", tiled=True)
    cone_expansions, lowfreq = pl.pallas_call(
        level_kernel,
        out_shape=[
            jax.ShapeDtypeStruct((cones, fours, width), f32),
            jax.ShapeDtypeStruct((8, width), f32),
        ],
        in_specs=[vmem()] * 7,
        out_specs=[vmem(), vmem()],
        compiler_params=pltpu.CompilerParams(vmem_limit_bytes=24 << 20),
        name="levels",
    )(here(gathered), *[here(table) for table in tables], weights)
    return (lowfreq, cone_expansions)


def solution(mesh):
    halves, blocks, subs = mesh.devices.shape
    fine = Mesh(
        mesh.devices.reshape(halves, blocks // OCTANTS, OCTANTS, subs), ("half", "z", "y", "sub")
    )
    blk = ("half", "z", "y")
    return jax.shard_map(
        local,
        mesh=fine,
        in_specs=(
            P(blk + ("sub",), None),
            P(blk + ("sub",)),
            P(),
            P(blk, "sub"),
            P(blk, "sub"),
        ),
        out_specs=(P(blk + ("sub",), None), P(blk, "sub", None)),
        check_vma=False,
    )
```
